512 devices in a mesh: group: 64 (over z, x, core), tensor: 8 (over y).
Axes of the slice: x: 4, y: 8, z: 8, core: 2. Of those that a mesh axis runs over, the one named last changes fastest.
Arguments:
- hidden: bfloat16 [32768, 2048], P(('group', 'tensor')), may hold values from -6 to 6
- norm_gain: bfloat16 [2048], replicated, may hold values from 0.099609375 to 1.8984375
- q_weight: bfloat16 [2048, 3072], P(None, 'tensor'), may hold values from -0.125 to 0.125
- latent_down_weight: bfloat16 [2048, 512], P(None, 'tensor'), may hold values from -0.125 to 0.125
- kva_rope: bfloat16 [2048, 64], replicated, may hold values from -0.125 to 0.125
- latent_norm_scale: bfloat16 [512], replicated, may hold values from 0.099609375 to 1.8984375
- key_value_up_weight: bfloat16 [512, 4096], P(None, 'tensor'), may hold values from -0.25 to 0.25
- earlier_token_cache: bfloat16 [65536, 576], P('group'), may hold values from -2400 to 2400
- span_lens: int32 [64, 8], P('group'), may hold values from 1 to 256, 512 in all within a row
- prior_lens: int32 [64, 8], P('group'), may hold values from 2 to 128, as said below
- old_cache: bfloat16 [2, 524288, 576], P(None, ('group', 'tensor')), may hold values from -6 to 6
- block_slot: int32 [512, 64], P(('group', 'tensor')), may hold values from 0 to 63, each once within a row
Outputs:
- attn_out: bfloat16 [32768, 2048], P('group', 'tensor')
- new_cache: bfloat16 [2, 524288, 576], P(None, 'group', 'tensor')
The draws below stay inside these ranges and needn't reach their ends.
Inputs may be any that keep to these rules, and one draw needn't show every extreme that they name: `prior_lens`: each row's values reach 128 in every group.
All inputs are finite; a program needn't handle non-finite values.
Results may differ from the reference program's by a relative error of at most 0.013.
The reference program's roundings to bfloat16 on the way count: a program that leaves them out, or rounds other values in their place, can miss the bound.
Values may be sent and summed in bfloat16 or wider, within the bound.
A program may use at most 128 MiB of HBM per device.

```python
import math
import jax
import jax.numpy as jnp
import numpy as np
from jax import lax

MODEL_WIDTH = 2048
ATTENTION_HEADS = 16
PLAIN_HEAD_SIZE = 128
ROTARY_SIZE = 64
VALUE_SIZE = 128
LATENT_WIDTH = 512
TOK_DEV = 512
REQ_GRP = 8
PRIOR_REQ = 128
LAYERS = 2
BLK_TOK = 16
BLK_DEV = 64
LAT = 576
TOKENS = 32768
SPAN_MOST = 256
PRIOR_GRP = 1024
MOVE_ROWS = 524288
N_GROUP = 64
N_TENSOR = 8
DEVICES = 512


def draw_earlier_token_cache(key, part):
    first_index = jax.random.fold_in(key, 0)
    token_rows = N_GROUP * PRIOR_GRP
    base_offset = jnp.clip(jax.random.normal(first_index, (token_rows, LATENT_WIDTH + ROTARY_SIZE), jnp.float32), -4.0, 4.0)
    return base_offset.astype(jnp.bfloat16)


def draw_prior_lens(key, part):
    first_index, second, third = jax.random.split(key, 3)
    factor = jax.random.randint(first_index, (N_GROUP, 1), 1, 5)
    raw = jax.random.randint(second, (N_GROUP, REQ_GRP), 0, PRIOR_REQ - 1)
    lens = 2 + raw * factor // 4
    pick = jax.random.randint(third, (N_GROUP, 1), 0, REQ_GRP)
    chosen = jnp.arange(REQ_GRP, dtype=jnp.int32)[None, :] == pick
    return jnp.where(chosen, PRIOR_REQ, lens).astype(jnp.int32)


def level_of(own_key, dims, cuts, low, largest):
    level, own = 1.0, jax.random.fold_in(own_key, 6)
    for dim, blocks in cuts:
        draws = jnp.exp(jax.random.uniform(jax.random.fold_in(own, dim), (blocks,), jnp.float32, low / len(cuts), largest / len(cuts)))
        level = level * jnp.repeat(draws, dims[dim] // blocks).reshape([-1 if axis == dim else 1 for axis in range(len(dims))])
    return level


def split_up(number_of, total, reach, skew):
    weights = [(1 << 20) // math.isqrt(rank ** skew) + 1 for rank in range(2, number_of + 1)]
    rest, holding = total - reach - (number_of - 1), [1] * (number_of - 1)
    while rest > 0:
        free = [i for i in range(number_of - 1) if holding[i] < reach]
        whole, left = sum([weights[i] for i in free]), rest
        for i in free:
            addition = min(reach - holding[i], max(1, left * weights[i] // whole), rest)
            holding[i] = holding[i] + addition
            rest = rest - addition
    return np.array([reach] + holding)


def uneven_parts(stream_key, count, total, most, skew):
    if count == 2:
        one = jax.random.randint(stream_key, (), max(1, total - most), min(most, total - 1) + 1)
        return jnp.stack([one, total - one])
    lengths = jnp.asarray(split_up(count, total, most, skew), jnp.int32)
    couples = (count - 1) // 2
    source_of, receiver = lengths[1:1 + 2 * couples:2], lengths[2:2 + 2 * couples:2]
    room = jnp.minimum(source_of - 1, most - receiver)
    moved = jax.random.randint(jax.random.fold_in(stream_key, 1), (couples,), 0, 1 << 20) % (room + 1)
    lengths = lengths.at[1:1 + 2 * couples:2].set(source_of - moved).at[2:2 + 2 * couples:2].set(receiver + moved)
    return lengths[jax.random.permutation(jax.random.fold_in(stream_key, 2), count)]


def normal_values(stream_key, extent, scale, limit, cuts=(), held_as=jnp.bfloat16):
    level = level_of(stream_key, extent, cuts, -0.22, 0.18) if cuts else 1.0
    drawn = jax.random.normal(stream_key, extent, jnp.float32) * scale * level
    return jnp.minimum(jnp.maximum(drawn, -limit), limit).astype(held_as)


def setup_inputs(seed: int = 0) -> dict:
    key_list = jax.random.split(jax.random.key(seed), 13)
    return {
        "hidden": normal_values(key_list[0], (TOKENS, MODEL_WIDTH), 1.0, 6.0, ((0, 512),)),
        "norm_gain": jnp.clip(1.0 + 0.18 * jax.random.normal(key_list[1], (MODEL_WIDTH,), jnp.float32), 0.099609375, 1.8984375).astype(jnp.bfloat16),
        "q_weight": normal_values(key_list[2], (MODEL_WIDTH, ATTENTION_HEADS * (PLAIN_HEAD_SIZE + ROTARY_SIZE)), MODEL_WIDTH ** -0.5, 0.125, ((1, 8),)),
        "latent_down_weight": normal_values(key_list[3], (MODEL_WIDTH, LATENT_WIDTH), MODEL_WIDTH ** -0.5, 0.125, ((1, 8),)),
        "kva_rope": normal_values(key_list[4], (MODEL_WIDTH, ROTARY_SIZE), MODEL_WIDTH ** -0.5, 0.125),
        "latent_norm_scale": jnp.clip(1.0 + 0.18 * jax.random.normal(key_list[5], (LATENT_WIDTH,), jnp.float32), 0.099609375, 1.8984375).astype(jnp.bfloat16),
        "key_value_up_weight": normal_values(key_list[6], (LATENT_WIDTH, ATTENTION_HEADS * (PLAIN_HEAD_SIZE + VALUE_SIZE)), LATENT_WIDTH ** -0.5, 0.25, ((1, 8),)),
        "earlier_token_cache": draw_earlier_token_cache(jax.random.fold_in(key_list[12], 71), 0),
        "span_lens": jax.vmap(lambda own: uneven_parts(own, REQ_GRP, TOK_DEV, SPAN_MOST, 2))(jax.random.split(key_list[8], N_GROUP)).reshape((N_GROUP, REQ_GRP)).astype(jnp.int32),
        "prior_lens": draw_prior_lens(jax.random.fold_in(key_list[12], 71), 0),
        "old_cache": normal_values(key_list[10], (LAYERS, MOVE_ROWS, LAT), 1.0, 6.0, ((1, 512),)),
        "block_slot": jax.vmap(lambda own: jax.random.permutation(own, BLK_DEV))(jax.random.split(key_list[11], DEVICES)).reshape((DEVICES, BLK_DEV)).astype(jnp.int32),
    }


EPS = 1e-06
ROPE_BASE = 10000.0

def rms_scale(values, gain):
    mean_sq = lax.optimization_barrier(jnp.mean(values * values, axis=-1, keepdims=True))
    return values * lax.rsqrt(mean_sq + EPS) * gain.astype(jnp.float32)

def rope_tables(position, width):
    half = width // 2
    freqs = ROPE_BASE ** (-(jnp.arange(half, dtype=jnp.float32) * 2.0) / float(width))
    angles = position.astype(jnp.float32)[:, None] * freqs[None, :]
    return (jnp.cos(angles), jnp.sin(angles))

def rotate(values, cosine, sine):
    half = values.shape[-1] // 2
    first_index = values[..., :half]
    second = values[..., half:]
    return jnp.concatenate([first_index * cosine - second * sine, second * cosine + first_index * sine], axis=-1)

def token_layout(lens, priors, count):
    ends = jnp.cumsum(lens).astype(jnp.int32)
    starts = ends - lens
    tokens = jnp.arange(count, dtype=jnp.int32)
    request = lax.optimization_barrier(jnp.sum((tokens[:, None] >= ends[None, :]).astype(jnp.int32), axis=1))
    onehot = request[:, None] == jnp.arange(lens.shape[0], dtype=jnp.int32)[None, :]
    start_of = lax.optimization_barrier(jnp.sum(jnp.where(onehot, starts[None, :], 0), axis=1)).astype(jnp.int32)
    prior_of = lax.optimization_barrier(jnp.sum(jnp.where(onehot, priors[None, :], 0), axis=1)).astype(jnp.int32)
    index = tokens - start_of
    return (request, index, prior_of, prior_of + index)

def allowed_keys(request, index, prior_of, prior_count, per_request):
    slots = jnp.arange(prior_count, dtype=jnp.int32)
    prior_ok = (request[:, None] == (slots // per_request)[None, :]) & ((slots % per_request)[None, :] < prior_of[:, None])
    new_ok = (request[:, None] == request[None, :]) & (index[None, :] <= index[:, None])
    return jnp.concatenate([prior_ok, new_ok], axis=1)

def group_attention(token_rows, lens, priors, earlier_cache_rows, norm_gain, q_weight, latent_down_weight, kva_rope, latent_norm_scale, key_value_up_weight):
    count = token_rows.shape[0]
    normed = rms_scale(token_rows.astype(jnp.float32), norm_gain).astype(jnp.bfloat16)
    request, index, prior_of, position = token_layout(lens, priors, count)
    cosine, sine = rope_tables(position, ROTARY_SIZE)
    query = jnp.dot(normed, q_weight, preferred_element_type=jnp.float32).reshape(count, ATTENTION_HEADS, PLAIN_HEAD_SIZE + ROTARY_SIZE)
    q_nope = query[..., :PLAIN_HEAD_SIZE].astype(jnp.bfloat16)
    q_pe = rotate(query[..., PLAIN_HEAD_SIZE:], cosine[:, None, :], sine[:, None, :]).astype(jnp.bfloat16)
    latent_state = rms_scale(jnp.dot(normed, latent_down_weight, preferred_element_type=jnp.float32), latent_norm_scale).astype(jnp.bfloat16)
    fresh_rotary_key = rotate(jnp.dot(normed, kva_rope, preferred_element_type=jnp.float32), cosine, sine).astype(jnp.bfloat16)
    latent_key_rows = jnp.concatenate([earlier_cache_rows[:, :LATENT_WIDTH], latent_state], axis=0)
    rotary_key_rows = jnp.concatenate([earlier_cache_rows[:, LATENT_WIDTH:], fresh_rotary_key], axis=0)
    keys = latent_key_rows.shape[0]
    expanded = jnp.dot(latent_key_rows, key_value_up_weight, preferred_element_type=jnp.float32).astype(jnp.bfloat16)
    expanded = expanded.reshape(keys, ATTENTION_HEADS, PLAIN_HEAD_SIZE + VALUE_SIZE)
    key_nope = expanded[..., :PLAIN_HEAD_SIZE]
    values = expanded[..., PLAIN_HEAD_SIZE:]
    scores = jnp.einsum('thd,khd->htk', q_nope.astype(jnp.float32), key_nope.astype(jnp.float32))
    scores = scores + jnp.einsum('thd,kd->htk', q_pe.astype(jnp.float32), rotary_key_rows.astype(jnp.float32))
    scores = scores * (PLAIN_HEAD_SIZE + ROTARY_SIZE) ** (-0.5)
    allowed = allowed_keys(request, index, prior_of, earlier_cache_rows.shape[0], PRIOR_REQ)[None]
    top = lax.optimization_barrier(jnp.max(jnp.where(allowed, scores, -jnp.inf), axis=-1, keepdims=True))
    weights = jnp.where(allowed, jnp.exp(scores - top), 0.0)
    total = lax.optimization_barrier(jnp.sum(weights, axis=-1, keepdims=True))
    probs = (weights / total).astype(jnp.bfloat16)
    mixed = jnp.einsum('htk,khd->thd', probs.astype(jnp.float32), values.astype(jnp.float32))
    return mixed.astype(jnp.bfloat16).reshape(count, ATTENTION_HEADS * VALUE_SIZE)

def move_blocks(old_cache, block_slot):
    sources = N_GROUP * N_TENSOR
    per = BLK_DEV // N_GROUP
    source = jnp.arange(sources, dtype=jnp.int32)[:, None]
    group_of = source // N_TENSOR
    tensor_of = source % N_TENSOR
    dest = block_slot // per * (N_TENSOR * N_GROUP * per) + (tensor_of * N_GROUP + group_of) * per + block_slot % per
    blocks = old_cache.reshape(LAYERS, sources * BLK_DEV, BLK_TOK, LAT)
    moved = jnp.zeros_like(blocks).at[:, dest.reshape(-1).astype(jnp.int32)].set(blocks)
    return moved.reshape(LAYERS, MOVE_ROWS, LAT)

def reference(hidden, norm_gain, q_weight, latent_down_weight, kva_rope, latent_norm_scale, key_value_up_weight, earlier_token_cache, span_lens, prior_lens, old_cache, block_slot):
    items = (hidden.reshape(N_GROUP, TOK_DEV, MODEL_WIDTH), span_lens, prior_lens, earlier_token_cache.reshape(N_GROUP, PRIOR_GRP, LAT))

    def one_group(item):
        return group_attention(item[0], item[1], item[2], item[3], norm_gain, q_weight, latent_down_weight, kva_rope, latent_norm_scale, key_value_up_weight)
    attn_out = lax.map(one_group, items).reshape(TOKENS, ATTENTION_HEADS * VALUE_SIZE)
    new_cache = move_blocks(old_cache, block_slot)
    return (attn_out, new_cache)
```

```python
import functools

import jax
import jax.numpy as jnp
from jax import lax
from jax.experimental import pallas as pl
from jax.experimental.pallas import tpu as pltpu
from jax.sharding import PartitionSpec as P

MESH = pl.DeviceIdType.MESH
PARTS = {"ag": True, "a": True, "b": True}


def move_kernel(slots_ref, hidden_ref, old_ref, rows_ref, new_ref,
                own, arranged, landed, mid, hall,
                load_sem, ag_send, ag_recv, a_send, a_recv, b_send, b_recv, out_sem):
    g = lax.axis_index("group")
    t = lax.axis_index("tensor")
    z, xc = g // 8, g % 8
    x, c = xc // 2, xc % 2

    def side(dx, dc):
        return lax.rem(x + dx, 4) * 2 + lax.rem(c + dc, 2)

    barrier = pltpu.get_barrier_semaphore()
    right, left = lax.rem(t + 1, 8), lax.rem(t + 7, 8)
    load = pltpu.make_async_copy(old_ref, own, load_sem.at[0])
    load.start()
    mine = pltpu.make_async_copy(hidden_ref, hall.at[t], load_sem.at[1])
    mine.start()
    for k in range(1, 8):
        pl.semaphore_signal(barrier, inc=1, device_id=(z * 8 + side(k // 2, k % 2), t), device_id_type=MESH)

    def greet(k, carry):
        zz, tt = lax.rem(z + k // 8, 8), lax.rem(t + k % 8, 8)
        pl.semaphore_signal(barrier, inc=1, device_id=(zz * 8 + xc, tt), device_id_type=MESH)
        return carry

    lax.fori_loop(1, 64, greet, 0)
    pl.semaphore_wait(barrier, 70)

    def hop(way, step, half):
        owner = lax.rem(t + (8 - step if way == 0 else step), 8)
        rows = pl.ds(half * 32, 32)
        src = hidden_ref.at[rows] if step == 0 else hall.at[owner, rows]
        return pltpu.make_async_remote_copy(
            src_ref=src, dst_ref=hall.at[owner, rows],
            send_sem=ag_send.at[way, step, half], recv_sem=ag_recv.at[way, step, half],
            device_id=(g, right if way == 0 else left), device_id_type=MESH)

    hops = [[(w, s, h) for h in (0, 1) for w in (0, 1) if s < 3 or h == w] for s in range(4)]
    if PARTS["ag"]:
        for w, s, h in hops[0]:
            hop(w, s, h).start()

    slots = slots_ref[...]
    spread = (lax.broadcasted_iota(jnp.int32, (64, 1024), 1) // 16
              == lax.broadcasted_iota(jnp.int32, (64, 1024), 0)).astype(jnp.bfloat16)
    slot_of = jnp.dot(slots.astype(jnp.float32).astype(jnp.bfloat16), spread, preferred_element_type=jnp.float32)[0:1]
    place_of = lax.broadcasted_iota(jnp.int32, (256, 1024), 1) % 16
    lane = lax.broadcasted_iota(jnp.int32, (256, 1024), 0)
    slot_of = jnp.broadcast_to(slot_of, (256, 1024)).astype(jnp.int32)
    load.wait()

    def a_copy(layer, k):
        to = side(k // 2, k % 2)
        return pltpu.make_async_remote_copy(
            src_ref=arranged.at[to, layer], dst_ref=landed.at[xc, layer],
            send_sem=a_send.at[layer, k], recv_sem=a_recv.at[layer, k],
            device_id=(z * 8 + to, t), device_id_type=MESH)

    picks = []
    for pair in range(4):
        want = (lane % 128) // 16 * 8 + pair * 2 + lane // 128
        picks.append(((slot_of == want) & (place_of == lane % 16)).astype(jnp.bfloat16))
    for layer in range(2):
        for pair in range(4):
            got = lax.dot_general(own[layer], picks[pair], (((1,), (1,)), ((), ())),
                                  preferred_element_type=jnp.float32).astype(jnp.bfloat16)
            arranged[2 * pair, layer] = got[:, :128]
            arranged[2 * pair + 1, layer] = got[:, 128:]
        if PARTS["a"]:
            for k in (4, 5, 2, 6, 3, 7, 1):
                a_copy(layer, k).start()
    stay = [pltpu.make_async_copy(arranged.at[xc, layer], landed.at[xc, layer], load_sem.at[2 + layer]) for layer in range(2)]
    for s in stay:
        s.start()

    if PARTS["ag"]:
        for s in range(4):
            for w, _, h in hops[s]:
                hop(w, s, h).wait_recv()
                if s < 3 and (w, s + 1, h) in hops[s + 1]:
                    hop(w, s + 1, h).start()
        for s in range(4):
            for w, _, h in hops[s]:
                hop(w, s, h).wait_send()
    mine.wait()
    rows_out = pltpu.make_async_copy(hall, rows_ref, out_sem.at[0])
    rows_out.start()

    col = lax.broadcasted_iota(jnp.int32, (1024, 256), 1)
    row = lax.broadcasted_iota(jnp.int32, (1024, 256), 0)
    swaps = [(row == (col % 128) // 16 * 128 + (pair * 2 + col // 128) * 16 + col % 16).astype(jnp.bfloat16)
             for pair in range(4)]

    def b_copy(layer, k):
        zz, tt = lax.rem(z + k // 8, 8), lax.rem(t + k % 8, 8)
        place = pl.ds(pl.multiple_of((t * 8 + z) * 128, 128), 128)
        return pltpu.make_async_remote_copy(
            src_ref=mid.at[zz, layer, tt], dst_ref=new_ref.at[layer, :, place],
            send_sem=b_send.at[layer, k], recv_sem=b_recv.at[layer, k],
            device_id=(zz * 8 + xc, tt), device_id_type=MESH)

    keeps = []
    for layer in range(2):
        stay[layer].wait()
        if PARTS["a"]:
            for k in range(1, 8):
                a_copy(layer, k).wait_recv()
        for pair in range(4):
            every = jnp.concatenate([landed[s, layer] for s in range(8)], axis=1)
            got = jnp.dot(every, swaps[pair], preferred_element_type=jnp.float32).astype(jnp.bfloat16)
            for u in range(8):
                mid[2 * pair, layer, u] = got[u * 72:(u + 1) * 72, :128]
                mid[2 * pair + 1, layer, u] = got[u * 72:(u + 1) * 72, 128:]

        if PARTS["b"]:
            def go(k, carry):
                b_copy(layer, k).start()
                return carry

            lax.fori_loop(1, 64, go, 0)
        place = pl.ds(pl.multiple_of((t * 8 + z) * 128, 128), 128)
        keep = pltpu.make_async_copy(mid.at[z, layer, t], new_ref.at[layer, :, place], out_sem.at[1 + layer])
        keep.start()
        keeps.append(keep)

    for layer in range(2):
        keeps[layer].wait()
        if PARTS["a"]:
            for k in range(1, 8):
                a_copy(layer, k).wait_send()
        if PARTS["b"]:
            def end(k, carry):
                copy = b_copy(layer, k)
                copy.wait_send()
                copy.wait_recv()
                return carry

            lax.fori_loop(1, 64, end, 0)
    rows_out.wait()


def move(slots, hidden, old):
    layers, width, rows = old.shape
    any_spec = pl.BlockSpec(memory_space=pl.ANY)
    bf = jnp.bfloat16
    dma = pltpu.SemaphoreType.DMA
    return pl.pallas_call(
        move_kernel,
        out_shape=(jax.ShapeDtypeStruct((8, 64, 2048), bf), jax.ShapeDtypeStruct((2, 72, 8192), bf)),
        in_specs=[pl.BlockSpec(memory_space=pltpu.VMEM), any_spec, any_spec],
        out_specs=(any_spec, any_spec),
        scratch_shapes=[
            pltpu.VMEM((2, 576, 1024), bf),
            pltpu.VMEM((8, 2, 576, 128), bf),
            pltpu.VMEM((8, 2, 576, 128), bf),
            pltpu.VMEM((8, 2, 8, 72, 128), bf),
            pltpu.VMEM((8, 64, 2048), bf),
            dma((4,)), dma((2, 4, 2)), dma((2, 4, 2)), dma((2, 8)), dma((2, 8)), dma((2, 64)), dma((2, 64)), dma((3,)),
        ],
        compiler_params=pltpu.CompilerParams(collective_id=0, has_side_effects=True, vmem_limit_bytes=56 << 20),
    )(slots, hidden, old)


PLAIN_HEAD_SIZE = 128
ROTARY_SIZE = 64
VALUE_SIZE = 128
PRIOR_REQ = 128


EPS = 1e-06
ROPE_BASE = 10000.0


def rms_scale(values, gain):
    mean_sq = jnp.mean(values * values, axis=-1, keepdims=True)
    return values * lax.rsqrt(mean_sq + EPS) * gain.astype(jnp.float32)


def rope_tables(position, width):
    half = width // 2
    freqs = ROPE_BASE ** (-(jnp.arange(half, dtype=jnp.float32) * 2.0) / float(width))
    angles = position.astype(jnp.float32)[:, None] * freqs[None, :]
    return (jnp.cos(angles), jnp.sin(angles))


def rotate(values, cosine, sine):
    half = values.shape[-1] // 2
    first_index = values[..., :half]
    second = values[..., half:]
    return jnp.concatenate(
        [first_index * cosine - second * sine, second * cosine + first_index * sine], axis=-1
    )


def token_layout(lens, priors, count):
    ends = jnp.cumsum(lens)
    starts = ends - lens
    tokens = jnp.arange(count, dtype=jnp.int32)
    request = jnp.sum((tokens[:, None] >= ends[None, :]).astype(jnp.int32), axis=1)
    onehot = request[:, None] == jnp.arange(lens.shape[0], dtype=jnp.int32)[None, :]
    start_of = jnp.sum(jnp.where(onehot, starts[None, :], 0), axis=1)
    prior_of = jnp.sum(jnp.where(onehot, priors[None, :], 0), axis=1)
    index = tokens - start_of
    return (request, index, prior_of, prior_of + index)


def allowed_keys(request, index, prior_of, prior_count, per_request):
    slots = jnp.arange(prior_count, dtype=jnp.int32)
    prior_ok = (request[:, None] == (slots // per_request)[None, :]) & (
        (slots % per_request)[None, :] < prior_of[:, None]
    )
    new_ok = (request[:, None] == request[None, :]) & (index[None, :] <= index[:, None])
    return jnp.concatenate([prior_ok, new_ok], axis=1)


def local(
    hidden,
    norm_gain,
    q_weight,
    latent_down_weight,
    kva_rope,
    latent_norm_scale,
    key_value_up_weight,
    earlier_token_cache,
    span_lens,
    prior_lens,
    old_cache,
    block_slot,
):
    slots = jnp.broadcast_to(block_slot, (8, block_slot.shape[1]))
    token_rows, moved = move(slots, hidden, jnp.swapaxes(old_cache, 1, 2))
    new_cache = jnp.swapaxes(moved, 1, 2)
    token_rows = token_rows.reshape(-1, hidden.shape[1])
    count = token_rows.shape[0]
    normed = rms_scale(token_rows.astype(jnp.float32), norm_gain).astype(jnp.bfloat16)
    request, index, prior_of, position = token_layout(span_lens[0], prior_lens[0], count)
    cosine, sine = rope_tables(position, ROTARY_SIZE)
    heads = q_weight.shape[1] // (PLAIN_HEAD_SIZE + ROTARY_SIZE)
    query = jnp.dot(normed, q_weight, preferred_element_type=jnp.float32).reshape(
        count, heads, PLAIN_HEAD_SIZE + ROTARY_SIZE
    )
    q_nope = query[..., :PLAIN_HEAD_SIZE].astype(jnp.bfloat16)
    q_pe = rotate(query[..., PLAIN_HEAD_SIZE:], cosine[:, None, :], sine[:, None, :]).astype(
        jnp.bfloat16
    )
    fresh_rotary_key = rotate(
        jnp.dot(normed, kva_rope, preferred_element_type=jnp.float32), cosine, sine
    ).astype(jnp.bfloat16)
    partial_latent = jnp.dot(normed, latent_down_weight, preferred_element_type=jnp.float32)
    whole_latent = lax.all_gather(partial_latent, "tensor", axis=1, tiled=True)
    latent_state = rms_scale(whole_latent, latent_norm_scale).astype(jnp.bfloat16)
    latent_columns = latent_state.shape[1]
    latent_key_rows = jnp.concatenate(
        [earlier_token_cache[:, :latent_columns], latent_state], axis=0
    )
    rotary_key_rows = jnp.concatenate(
        [earlier_token_cache[:, latent_columns:], fresh_rotary_key], axis=0
    )
    keys = latent_key_rows.shape[0]
    expanded = jnp.dot(
        latent_key_rows, key_value_up_weight, preferred_element_type=jnp.float32
    ).astype(jnp.bfloat16)
    expanded = expanded.reshape(keys, heads, PLAIN_HEAD_SIZE + VALUE_SIZE)
    key_nope = expanded[..., :PLAIN_HEAD_SIZE]
    values = expanded[..., PLAIN_HEAD_SIZE:]
    scores = jnp.einsum("thd,khd->htk", q_nope, key_nope, preferred_element_type=jnp.float32)
    scores = scores + jnp.einsum(
        "thd,kd->htk", q_pe, rotary_key_rows, preferred_element_type=jnp.float32
    )
    scores = scores * (PLAIN_HEAD_SIZE + ROTARY_SIZE) ** (-0.5)
    allowed = allowed_keys(request, index, prior_of, earlier_token_cache.shape[0], PRIOR_REQ)[None]
    top = jnp.max(jnp.where(allowed, scores, -jnp.inf), axis=-1, keepdims=True)
    weights = jnp.where(allowed, jnp.exp(scores - top), 0.0)
    total = jnp.sum(weights, axis=-1, keepdims=True)
    probs = (weights / total).astype(jnp.bfloat16)
    mixed = jnp.einsum("htk,khd->thd", probs, values, preferred_element_type=jnp.float32)
    attn_out = mixed.astype(jnp.bfloat16).reshape(count, heads * VALUE_SIZE)
    return (attn_out, new_cache)


def solution(mesh):
    in_specs = (
        P(("group", "tensor"), None),
        P(),
        P(None, "tensor"),
        P(None, "tensor"),
        P(),
        P(),
        P(None, "tensor"),
        P("group", None),
        P("group", None),
        P("group", None),
        P(None, ("group", "tensor"), None),
        P(("group", "tensor"), None),
    )
    out_specs = (P("group", "tensor"), P(None, "group", "tensor"))
    return jax.shard_map(local, mesh=mesh, in_specs=in_specs, out_specs=out_specs, check_vma=False)
```

```python
import jax
import jax.numpy as jnp
from jax import lax
from jax.experimental import pallas as pl
from jax.experimental.pallas import tpu as pltpu
from jax.sharding import PartitionSpec as P

MESH = pl.DeviceIdType.MESH
BF = jnp.bfloat16
F32 = jnp.float32
EPS = 1e-06
LOG_BASE = 9.210340371976184
SCALE = 192 ** (-0.5)


def layer_kernel(slots_ref, span_ref, prior_ref, gain_ref, scale_ref,
                 hidden_ref, old_ref, qw_ref, latw_ref, kva_ref, up_ref, cache_ref,
                 attn_ref, new_ref,
                 own, arranged, landed, mid, hall, nrm, qw, wlk, up, cache, keys, vals, qcat, latall,
                 load_sem, ag_send, ag_recv, a_send, a_recv, b_send, b_recv, l_send, l_recv, out_sem):
    g = lax.axis_index("group")
    t = lax.axis_index("tensor")
    z, xc = g // 8, g % 8
    x, c = xc // 2, xc % 2
    right, left = lax.rem(t + 1, 8), lax.rem(t + 7, 8)

    def side(k):
        return lax.rem(x + k // 2, 4) * 2 + lax.rem(c + k % 2, 2)

    loads = [pltpu.make_async_copy(src, dst, load_sem.at[i]) for i, (src, dst) in enumerate([
        (old_ref, own), (hidden_ref, hall.at[t]), (up_ref, up), (cache_ref, cache),
        (latw_ref, wlk.at[0:64]), (kva_ref, wlk.at[64:128]), (qw_ref, qw)])]
    for load in loads:
        load.start()

    barrier = pltpu.get_barrier_semaphore()
    for k in range(1, 8):
        pl.semaphore_signal(barrier, inc=1, device_id=(z * 8 + side(k), t), device_id_type=MESH)

    def greet(k, carry):
        zz, tt = lax.rem(z + k // 8, 8), lax.rem(t + k % 8, 8)
        pl.semaphore_signal(barrier, inc=1, device_id=(zz * 8 + xc, tt), device_id_type=MESH)
        return carry

    lax.fori_loop(1, 64, greet, 0)
    pl.semaphore_wait(barrier, 70)

    def hop(way, step, half):
        owner = lax.rem(t + (8 - step if way == 0 else step), 8)
        rows = pl.ds(half * 32, 32)
        src = hidden_ref.at[rows] if step == 0 else hall.at[owner, rows]
        return pltpu.make_async_remote_copy(
            src_ref=src, dst_ref=hall.at[owner, rows],
            send_sem=ag_send.at[way, step, half], recv_sem=ag_recv.at[way, step, half],
            device_id=(g, right if way == 0 else left), device_id_type=MESH)

    hops = [[(w, s, h) for h in (0, 1) for w in (0, 1) if s < 3 or h == w] for s in range(4)]

    def pass_on(s):
        for w, _, h in hops[s]:
            hop(w, s, h).wait_recv()
            if s < 3 and (w, s + 1, h) in hops[s + 1]:
                hop(w, s + 1, h).start()

    for w, s, h in hops[0]:
        hop(w, s, h).start()

    slots = jnp.broadcast_to(slots_ref[...], (8, 64))
    spread = (lax.broadcasted_iota(jnp.int32, (64, 1024), 1) // 16
              == lax.broadcasted_iota(jnp.int32, (64, 1024), 0)).astype(BF)
    slot_of = jnp.dot(slots.astype(F32).astype(BF), spread, preferred_element_type=F32)[0:1]
    slot_of = jnp.broadcast_to(slot_of, (256, 1024)).astype(jnp.int32)
    place_of = lax.broadcasted_iota(jnp.int32, (256, 1024), 1) % 16
    lane = lax.broadcasted_iota(jnp.int32, (256, 1024), 0)

    def a_copy(layer, k):
        return pltpu.make_async_remote_copy(
            src_ref=arranged.at[side(k), layer], dst_ref=landed.at[xc, layer],
            send_sem=a_send.at[layer, k], recv_sem=a_recv.at[layer, k],
            device_id=(z * 8 + side(k), t), device_id_type=MESH)

    picks = []
    for pair in range(4):
        want = (lane % 128) // 16 * 8 + pair * 2 + lane // 128
        picks.append(((slot_of == want) & (place_of == lane % 16)).astype(BF))
    loads[0].wait()
    stay = []
    for layer in range(2):
        for pair in range(4):
            got = lax.dot_general(own[layer], picks[pair], (((1,), (1,)), ((), ())),
                                  preferred_element_type=F32).astype(BF)
            arranged[2 * pair, layer] = got[:, :128]
            arranged[2 * pair + 1, layer] = got[:, 128:]
        for k in (4, 5, 2, 6, 3, 7, 1):
            a_copy(layer, k).start()
        stay.append(pltpu.make_async_copy(arranged.at[xc, layer], landed.at[xc, layer], out_sem.at[layer]))
        stay[layer].start()

    gain = gain_ref[...].astype(F32)

    def norm_rows(owner):
        rows = hall[owner].astype(F32)
        mean_sq = jnp.mean(rows * rows, axis=-1, keepdims=True)
        nrm[owner] = (rows * lax.rsqrt(mean_sq + EPS) * gain).astype(BF)

    loads[1].wait()
    norm_rows(t)
    pass_on(0)
    for load in loads[2:4]:
        load.wait()
    up_t = jnp.transpose(up[...].astype(F32)).astype(BF)

    def expand(latent_t, cols):
        wide = jnp.dot(up_t, latent_t, preferred_element_type=F32).astype(BF)
        for head in range(2):
            keys[head, 0:128, cols] = wide[head * 256:head * 256 + 128]
            vals[head, :, cols] = wide[head * 256 + 128:head * 256 + 256]

    for part in range(2):
        cols = slice(part * 512, part * 512 + 512)
        expand(cache[0:512, cols], cols)
        for head in range(2):
            keys[head, 128:192, cols] = cache[512:576, cols]
            keys[head, 192:256, cols] = cache[512:576, cols]
    norm_rows(left)
    norm_rows(right)
    pass_on(1)

    spans = [span_ref[0, r] for r in range(8)]
    priors = [prior_ref[0, r] for r in range(8)]
    starts = [jnp.int32(0)]
    for r in range(7):
        starts.append(starts[r] + spans[r])

    def places(token):
        start, prior, request = jnp.zeros_like(token), jnp.zeros_like(token) + priors[0], jnp.zeros_like(token)
        for r in range(1, 8):
            inside = token >= starts[r]
            start = jnp.where(inside, starts[r], start)
            prior = jnp.where(inside, priors[r], prior)
            request = jnp.where(inside, r, request)
        return start, prior, request

    token = lax.broadcasted_iota(jnp.int32, (32, 512), 1)
    start, prior, _ = places(token)
    position = (prior + token - start).astype(F32)
    pair_of = lax.broadcasted_iota(jnp.int32, (32, 512), 0).astype(F32)
    angle = position * jnp.exp(pair_of * (-2.0 / 64 * LOG_BASE))
    cosine, sine = jnp.cos(angle), jnp.sin(angle)

    def rotate(rows):
        first, second = rows[0:32], rows[32:64]
        return [first * cosine - second * sine, second * cosine + first * sine]

    norm_rows(lax.rem(t + 6, 8))
    norm_rows(lax.rem(t + 2, 8))
    pass_on(2)
    norm_rows(lax.rem(t + 5, 8))
    norm_rows(lax.rem(t + 3, 8))
    pass_on(3)
    norm_rows(lax.rem(t + 4, 8))

    normed = nrm[...].reshape(512, 2048)
    for load in loads[4:6]:
        load.wait()
    small = lax.dot_general(wlk[...], normed, (((1,), (1,)), ((), ())), preferred_element_type=F32)
    latall[t] = small[0:64].astype(BF)
    rotary_new = jnp.concatenate(rotate(small[64:128]), axis=0).astype(BF)
    for head in range(2):
        keys[head, 128:192, 1024:1536] = rotary_new
        keys[head, 192:256, 1024:1536] = rotary_new

    def l_copy(k):
        return pltpu.make_async_remote_copy(
            src_ref=latall.at[t], dst_ref=latall.at[t],
            send_sem=l_send.at[k], recv_sem=l_recv.at[k],
            device_id=(g, lax.rem(t + k, 8)), device_id_type=MESH)

    for k in (4, 3, 5, 2, 6, 1, 7):
        l_copy(k).start()

    col = lax.broadcasted_iota(jnp.int32, (1024, 256), 1)
    row = lax.broadcasted_iota(jnp.int32, (1024, 256), 0)
    swaps = [(row == (col % 128) // 16 * 128 + (pair * 2 + col // 128) * 16 + col % 16).astype(BF)
             for pair in range(4)]
    place = pl.ds(pl.multiple_of((t * 8 + z) * 128, 128), 128)

    def b_copy(layer, dz, dt):
        zz, tt = lax.rem(z + dz, 8), lax.rem(t + dt, 8)
        return pltpu.make_async_remote_copy(
            src_ref=mid.at[zz, layer, tt], dst_ref=new_ref.at[layer, :, place],
            send_sem=b_send.at[layer, dz * 8 + dt], recv_sem=b_recv.at[layer, dz * 8 + dt],
            device_id=(zz * 8 + xc, tt), device_id_type=MESH)

    keeps = []
    for layer in range(2):
        stay[layer].wait()
        for k in range(1, 8):
            a_copy(layer, k).wait_recv()
        every = jnp.concatenate([landed[s, layer] for s in range(8)], axis=1)
        for pair in range(4):
            got = jnp.dot(every, swaps[pair], preferred_element_type=F32).astype(BF)
            for u in range(8):
                mid[2 * pair, layer, u] = got[u * 72:(u + 1) * 72, :128]
                mid[2 * pair + 1, layer, u] = got[u * 72:(u + 1) * 72, 128:]

        def go(i, carry):
            far = (i >= 12).astype(jnp.int32)
            p = 1 + i // 4
            q = lax.rem(i, 4) + far
            for dz, dt in ((p, q), (8 - p, lax.rem(8 - q, 8)), (q, 8 - p), (lax.rem(8 - q, 8), p)):
                b_copy(layer, dz, dt).start()
            return carry

        lax.fori_loop(0, 15, go, 0)
        for dz, dt in ((4, 0), (0, 4), (4, 4)):
            b_copy(layer, dz, dt).start()
        keep = pltpu.make_async_copy(mid.at[z, layer, t], new_ref.at[layer, :, place], out_sem.at[2 + layer])
        keep.start()
        keeps.append(keep)

    loads[6].wait()
    query = jnp.dot(normed, qw[...], preferred_element_type=F32)
    turned = jnp.transpose(jnp.concatenate([query[:, 128:192], query[:, 320:384]], axis=1))
    turned = jnp.transpose(jnp.concatenate(rotate(turned[0:64]) + rotate(turned[64:128]), axis=0))
    half = lax.broadcasted_iota(jnp.int32, (512, 128), 1) // 64
    for head in range(2):
        qcat[head, :, 0:128] = query[:, head * 192:head * 192 + 128].astype(BF)
        qcat[head, :, 128:256] = jnp.where(half == head, turned, 0.0).astype(BF)

    for k in range(1, 8):
        l_copy(k).wait_recv()
    latent = latall[...].reshape(512, 512).astype(F32)
    mean_sq = jnp.mean(latent * latent, axis=0, keepdims=True)
    scale = jnp.transpose(jnp.broadcast_to(scale_ref[...].astype(F32), (128, 512)))
    scale = jnp.concatenate([scale] * 4, axis=1)
    expand((latent * lax.rsqrt(mean_sq + EPS) * scale).astype(BF), slice(1024, 1536))

    def attend(block, carry):
        rows = pl.ds(pl.multiple_of(block * 128, 128), 128)
        mine = lax.broadcasted_iota(jnp.int32, (128, 1), 0) + block * 128
        start, prior, request = places(mine)
        key = lax.broadcasted_iota(jnp.int32, (128, 1536), 1)
        allowed = ((key >= request * 128) & (key < request * 128 + prior)) | (
            (key >= start + 1024) & (key <= mine + 1024))
        for head in range(2):
            scores = jnp.dot(qcat[head, rows, :], keys[head], preferred_element_type=F32) * SCALE
            scores = jnp.where(allowed, scores, -jnp.inf)
            weights = jnp.exp(scores - jnp.max(scores, axis=-1, keepdims=True))
            probs = (weights / jnp.sum(weights, axis=-1, keepdims=True)).astype(BF)
            mixed = lax.dot_general(probs, vals[head], (((1,), (1,)), ((), ())), preferred_element_type=F32)
            attn_ref[rows, head * 128:head * 128 + 128] = mixed.astype(BF)
        return carry

    lax.fori_loop(0, 4, attend, 0)

    for s in range(4):
        for w, _, h in hops[s]:
            hop(w, s, h).wait_send()
    for k in range(1, 8):
        l_copy(k).wait_send()
    for layer in range(2):
        keeps[layer].wait()
        for k in range(1, 8):
            a_copy(layer, k).wait_send()

        def end(k, carry):
            copy = b_copy(layer, k // 8, lax.rem(k, 8))
            copy.wait_send()
            copy.wait_recv()
            return carry

        lax.fori_loop(1, 64, end, 0)


def local(hidden, norm_gain, q_weight, latent_down_weight, kva_rope, latent_norm_scale,
          key_value_up_weight, earlier_token_cache, span_lens, prior_lens, old_cache, block_slot):
    whole = pl.BlockSpec(memory_space=pl.ANY)
    vmem = pl.BlockSpec(memory_space=pltpu.VMEM)
    smem = pl.BlockSpec(memory_space=pltpu.SMEM)
    dma = pltpu.SemaphoreType.DMA
    attn_out, moved = pl.pallas_call(
        layer_kernel,
        out_shape=(jax.ShapeDtypeStruct((512, 256), BF), jax.ShapeDtypeStruct((2, 72, 8192), BF)),
        in_specs=[vmem, smem, smem, vmem, vmem] + [whole] * 7,
        out_specs=(vmem, whole),
        scratch_shapes=[
            pltpu.VMEM((2, 576, 1024), BF),
            pltpu.VMEM((8, 2, 576, 128), BF),
            pltpu.VMEM((8, 2, 576, 128), BF),
            pltpu.VMEM((8, 2, 8, 72, 128), BF),
            pltpu.VMEM((8, 64, 2048), BF),
            pltpu.VMEM((8, 64, 2048), BF),
            pltpu.VMEM((2048, 384), BF),
            pltpu.VMEM((128, 2048), BF),
            pltpu.VMEM((512, 512), BF),
            pltpu.VMEM((576, 1024), BF),
            pltpu.VMEM((2, 256, 1536), BF),
            pltpu.VMEM((2, 128, 1536), BF),
            pltpu.VMEM((2, 512, 256), BF),
            pltpu.VMEM((8, 64, 512), BF),
            dma((7,)), dma((2, 4, 2)), dma((2, 4, 2)), dma((2, 8)), dma((2, 8)), dma((2, 64)), dma((2, 64)),
            dma((8,)), dma((8,)), dma((4,)),
        ],
        compiler_params=pltpu.CompilerParams(collective_id=0, has_side_effects=True, vmem_limit_bytes=56 << 20),
    )(
        block_slot, span_lens, prior_lens, norm_gain[None], latent_norm_scale[None],
        hidden, jnp.swapaxes(old_cache, 1, 2), q_weight, latent_down_weight.T, kva_rope.T,
        key_value_up_weight, earlier_token_cache.T,
    )
    return attn_out, jnp.swapaxes(moved, 1, 2)


def solution(mesh):
    in_specs = (
        P(("group", "tensor"), None),
        P(),
        P(None, "tensor"),
        P(None, "tensor"),
        P(),
        P(),
        P(None, "tensor"),
        P("group", None),
        P("group", None),
        P("group", None),
        P(None, ("group", "tensor"), None),
        P(("group", "tensor"), None),
    )
    out_specs = (P("group", "tensor"), P(None, "group", "tensor"))
    return jax.shard_map(local, mesh=mesh, in_specs=in_specs, out_specs=out_specs, check_vma=False)
```

```python
import jax
import jax.numpy as jnp
from jax import lax
from jax.experimental import pallas as pl
from jax.experimental.pallas import tpu as pltpu
from jax.sharding import PartitionSpec as P

MESH = pl.DeviceIdType.MESH
BF = jnp.bfloat16
F32 = jnp.float32
EPS = 1e-06
LOG_BASE = 9.210340371976184
SCALE = 192 ** (-0.5)


def layer_kernel(slots_ref, span_ref, prior_ref, gain_ref, scale_ref,
                 hidden_ref, old_ref, qw_ref, latw_ref, kva_ref, up_ref, cache_ref,
                 attn_ref, new_ref,
                 own, arranged, landed, mid, hall, nrm, qw, kva, up, cache, keys, vals, qcat, wall, pick, swap,
                 load_sem, ag_send, ag_recv, a_send, a_recv, b_send, b_recv, w_send, w_recv, out_sem):
    g = lax.axis_index("group")
    t = lax.axis_index("tensor")
    z, xc = g // 8, g % 8
    x, c = xc // 2, xc % 2
    right, left = lax.rem(t + 1, 8), lax.rem(t + 7, 8)

    def side(k):
        return lax.rem(x + k // 2, 4) * 2 + lax.rem(c + k % 2, 2)

    piece = pl.ds(pl.multiple_of((z * 2 + c) * 128, 128), 128)
    loads = [pltpu.make_async_copy(src, dst, load_sem.at[i]) for i, (src, dst) in enumerate([
        (old_ref, own), (hidden_ref, hall.at[t]), (up_ref, up), (cache_ref, cache),
        (latw_ref.at[:, piece], wall.at[t, :, piece]), (kva_ref, kva), (qw_ref, qw)])]
    for load in loads:
        load.start()

    barrier = pltpu.get_barrier_semaphore()
    for k in range(1, 8):
        pl.semaphore_signal(barrier, inc=1, device_id=(z * 8 + side(k), t), device_id_type=MESH)

    def greet(k, carry):
        zz, tt = lax.rem(z + k // 8, 8), lax.rem(t + k % 8, 8)
        pl.semaphore_signal(barrier, inc=1, device_id=(zz * 8 + xc, tt), device_id_type=MESH)
        return carry

    lax.fori_loop(1, 64, greet, 0)
    pl.semaphore_wait(barrier, 70)

    def hop(way, step, half):
        owner = lax.rem(t + (8 - step if way == 0 else step), 8)
        rows = pl.ds(half * 32, 32)
        src = hidden_ref.at[rows] if step == 0 else hall.at[owner, rows]
        return pltpu.make_async_remote_copy(
            src_ref=src, dst_ref=hall.at[owner, rows],
            send_sem=ag_send.at[way, step, half], recv_sem=ag_recv.at[way, step, half],
            device_id=(g, right if way == 0 else left), device_id_type=MESH)

    hops = [[(w, s, h) for h in (0, 1) for w in (0, 1) if s < 3 or h == w] for s in range(4)]

    def pass_on(s):
        for w, _, h in hops[s]:
            hop(w, s, h).wait_recv()
            if s < 3 and (w, s + 1, h) in hops[s + 1]:
                hop(w, s + 1, h).start()

    for w, s, h in hops[0]:
        hop(w, s, h).start()

    def w_copy(stage, k):
        if stage == 0:
            peer, src, dst = (g, lax.rem(t + k, 8)), latw_ref.at[:, piece], wall.at[t, :, piece]
        elif stage == 1:
            peer, src, dst = (lax.rem(z + k, 8) * 8 + xc, t), wall.at[:, :, piece], wall.at[:, :, piece]
        else:
            cols = pl.ds(pl.multiple_of((lax.rem(z + 8 - k, 8) * 2 + c) * 128, 128), 128)
            peer, src, dst = (z * 8 + side(1), t), wall.at[:, :, cols], wall.at[:, :, cols]
        return pltpu.make_async_remote_copy(
            src_ref=src, dst_ref=dst, send_sem=w_send.at[stage, k], recv_sem=w_recv.at[stage, k],
            device_id=peer, device_id_type=MESH)

    for k in (4, 3, 5, 2, 6, 1, 7):
        w_copy(0, k).start()

    slots = jnp.broadcast_to(slots_ref[...], (8, 64))
    spread = (lax.broadcasted_iota(jnp.int32, (64, 1024), 1) // 16
              == lax.broadcasted_iota(jnp.int32, (64, 1024), 0)).astype(BF)
    slot_of = jnp.dot(slots.astype(F32).astype(BF), spread, preferred_element_type=F32)[0:1].astype(jnp.int32)
    code_of = slot_of * 16 + lax.broadcasted_iota(jnp.int32, (1, 1024), 1) % 16
    code_of = jnp.broadcast_to(code_of, (256, 1024))
    lane = lax.broadcasted_iota(jnp.int32, (256, 1), 0)

    seat = pl.ds(pl.multiple_of(xc * 128, 128), 128)

    def a_copy(layer, k):
        return pltpu.make_async_remote_copy(
            src_ref=arranged.at[side(k), layer], dst_ref=landed.at[layer, :, seat],
            send_sem=a_send.at[layer, k], recv_sem=a_recv.at[layer, k],
            device_id=(z * 8 + side(k), t), device_id_type=MESH)

    loads[0].wait()
    stay = []
    for pair in range(4):
        want = ((lane % 128) // 16 * 8 + pair * 2 + lane // 128) * 16 + lane % 16
        pick[pair] = (code_of == jnp.broadcast_to(want, (256, 1024))).astype(BF)
    for layer in range(2):
        for pair in range(4):
            got = lax.dot_general(own[layer], pick[pair], (((1,), (1,)), ((), ())),
                                  preferred_element_type=F32).astype(BF)
            arranged[2 * pair, layer] = got[:, :128]
            arranged[2 * pair + 1, layer] = got[:, 128:]
        for k in (4, 5, 2, 6, 3, 7, 1):
            a_copy(layer, k).start()
        stay.append(pltpu.make_async_copy(arranged.at[xc, layer], landed.at[layer, :, seat], out_sem.at[layer]))
        stay[layer].start()
        if layer == 0:
            pass_on(0)
            loads[4].wait()
            for k in range(1, 8):
                w_copy(0, k).wait_recv()
            for k in (4, 3, 5, 2, 6, 1, 7):
                w_copy(1, k).start()

    gain = gain_ref[...].reshape(1, 2048).astype(F32)

    def norm_rows(owner):
        rows = hall[owner].astype(F32)
        mean_sq = jnp.mean(rows * rows, axis=-1, keepdims=True)
        nrm[owner] = (rows * lax.rsqrt(mean_sq + EPS) * gain).astype(BF)

    row = lax.broadcasted_iota(jnp.int32, (1024, 256), 0)
    col = lax.broadcasted_iota(jnp.int32, (1, 256), 1)
    for pair in range(4):
        want = (col % 128) // 16 * 128 + (pair * 2 + col // 128) * 16 + col % 16
        swap[pair] = (row == jnp.broadcast_to(want, (1024, 256))).astype(BF)
    pass_on(1)
    loads[1].wait()
    norm_rows(t)
    norm_rows(left)
    norm_rows(right)
    norm_rows(lax.rem(t + 6, 8))
    norm_rows(lax.rem(t + 2, 8))
    pass_on(2)

    place = pl.ds(pl.multiple_of((t * 8 + z) * 128, 128), 128)

    def b_copy(layer, dz, dt):
        zz, tt = lax.rem(z + dz, 8), lax.rem(t + dt, 8)
        return pltpu.make_async_remote_copy(
            src_ref=mid.at[zz, layer, tt], dst_ref=new_ref.at[layer, :, place],
            send_sem=b_send.at[layer, dz * 8 + dt], recv_sem=b_recv.at[layer, dz * 8 + dt],
            device_id=(zz * 8 + xc, tt), device_id_type=MESH)

    keeps = []

    def send_layer(layer):
        stay[layer].wait()
        for k in range(1, 8):
            a_copy(layer, k).wait_recv()
        for pair in range(4):
            got = jnp.dot(landed[layer], swap[pair], preferred_element_type=F32).astype(BF)
            for u in range(8):
                mid[2 * pair, layer, u] = got[u * 72:(u + 1) * 72, :128]
                mid[2 * pair + 1, layer, u] = got[u * 72:(u + 1) * 72, 128:]

        def go(i, carry):
            far = (i >= 12).astype(jnp.int32)
            p = 1 + i // 4
            q = lax.rem(i, 4) + far
            for dz, dt in ((p, q), (8 - p, lax.rem(8 - q, 8)), (q, 8 - p), (lax.rem(8 - q, 8), p)):
                b_copy(layer, dz, dt).start()
            return carry

        lax.fori_loop(0, 15, go, 0)
        for dz, dt in ((4, 0), (0, 4), (4, 4)):
            b_copy(layer, dz, dt).start()
        keep = pltpu.make_async_copy(mid.at[z, layer, t], new_ref.at[layer, :, place], out_sem.at[2 + layer])
        keep.start()
        keeps.append(keep)

    send_layer(0)
    norm_rows(lax.rem(t + 5, 8))
    norm_rows(lax.rem(t + 3, 8))
    pass_on(3)
    norm_rows(lax.rem(t + 4, 8))

    normed = nrm[...].reshape(512, 2048)
    send_layer(1)
    w_copy(2, 0).start()
    for k in (1, 7, 2, 6, 3, 5, 4):
        w_copy(1, k).wait_recv()
        w_copy(2, k).start()

    for load in loads[2:4]:
        load.wait()
    up_t = jnp.transpose(up[...].astype(F32)).astype(BF)

    def expand(latent_t, cols):
        wide = jnp.dot(up_t, latent_t, preferred_element_type=F32).astype(BF)
        for head in range(2):
            keys[head, 0:128, cols] = wide[head * 256:head * 256 + 128]
            vals[head, :, cols] = wide[head * 256 + 128:head * 256 + 256]

    for part in range(2):
        cols = slice(part * 512, part * 512 + 512)
        expand(cache[0:512, cols], cols)
        for head in range(2):
            keys[head, 128:192, cols] = cache[512:576, cols]
            keys[head, 192:256, cols] = cache[512:576, cols]

    spans = [span_ref[0, r] for r in range(8)]
    priors = [prior_ref[0, r] for r in range(8)]
    starts = [jnp.int32(0)]
    for r in range(7):
        starts.append(starts[r] + spans[r])

    def places(token):
        start, prior, request = jnp.zeros_like(token), jnp.zeros_like(token) + priors[0], jnp.zeros_like(token)
        for r in range(1, 8):
            inside = token >= starts[r]
            start = jnp.where(inside, starts[r], start)
            prior = jnp.where(inside, priors[r], prior)
            request = jnp.where(inside, r, request)
        return start, prior, request

    token = lax.broadcasted_iota(jnp.int32, (32, 512), 1)
    start, prior, _ = places(token)
    position = (prior + token - start).astype(F32)
    pair_of = lax.broadcasted_iota(jnp.int32, (32, 512), 0).astype(F32)
    angle = position * jnp.exp(pair_of * (-2.0 / 64 * LOG_BASE))
    cosine, sine = jnp.cos(angle), jnp.sin(angle)

    def rotate(rows):
        first, second = rows[0:32], rows[32:64]
        return [first * cosine - second * sine, second * cosine + first * sine]

    loads[5].wait()
    rotary_new = lax.dot_general(kva[...], normed, (((1,), (1,)), ((), ())), preferred_element_type=F32)
    rotary_new = jnp.concatenate(rotate(rotary_new), axis=0).astype(BF)
    for head in range(2):
        keys[head, 128:192, 1024:1536] = rotary_new
        keys[head, 192:256, 1024:1536] = rotary_new

    loads[6].wait()
    query = jnp.dot(normed, qw[...], preferred_element_type=F32)
    turned = jnp.transpose(jnp.concatenate([query[:, 128:192], query[:, 320:384]], axis=1))
    turned = jnp.transpose(jnp.concatenate(rotate(turned[0:64]) + rotate(turned[64:128]), axis=0))
    half = lax.broadcasted_iota(jnp.int32, (512, 128), 1) // 64
    for head in range(2):
        qcat[head, :, 0:128] = query[:, head * 192:head * 192 + 128].astype(BF)
        qcat[head, :, 128:256] = jnp.where(half == head, turned, 0.0).astype(BF)

    for k in range(8):
        w_copy(2, k).wait_recv()
    latent = lax.dot_general(wall[...].reshape(512, 2048), normed, (((1,), (1,)), ((), ())),
                             preferred_element_type=F32)
    mean_sq = jnp.mean(latent * latent, axis=0, keepdims=True)
    scale = jnp.transpose(jnp.broadcast_to(scale_ref[...].reshape(1, 512).astype(F32), (128, 512)))
    scale = jnp.concatenate([scale] * 4, axis=1)
    expand((latent * lax.rsqrt(mean_sq + EPS) * scale).astype(BF), slice(1024, 1536))

    def attend(block, carry):
        rows = pl.ds(pl.multiple_of(block * 128, 128), 128)
        mine = lax.broadcasted_iota(jnp.int32, (128, 1), 0) + block * 128
        start, prior, request = places(mine)
        key = lax.broadcasted_iota(jnp.int32, (128, 1536), 1)
        allowed = ((key >= request * 128) & (key < request * 128 + prior)) | (
            (key >= start + 1024) & (key <= mine + 1024))
        for head in range(2):
            scores = jnp.dot(qcat[head, rows, :], keys[head], preferred_element_type=F32) * SCALE
            scores = jnp.where(allowed, scores, -jnp.inf)
            weights = jnp.exp(scores - jnp.max(scores, axis=-1, keepdims=True))
            probs = (weights / jnp.sum(weights, axis=-1, keepdims=True)).astype(BF)
            mixed = lax.dot_general(probs, vals[head], (((1,), (1,)), ((), ())), preferred_element_type=F32)
            attn_ref[rows, head * 128:head * 128 + 128] = mixed.astype(BF)
        return carry

    lax.fori_loop(0, 4, attend, 0)

    for s in range(4):
        for w, _, h in hops[s]:
            hop(w, s, h).wait_send()
    for stage in range(3):
        for k in range(1 if stage < 2 else 0, 8):
            w_copy(stage, k).wait_send()
    for layer in range(2):
        keeps[layer].wait()
        for k in range(1, 8):
            a_copy(layer, k).wait_send()

        def end(k, carry):
            copy = b_copy(layer, k // 8, lax.rem(k, 8))
            copy.wait_send()
            copy.wait_recv()
            return carry

        lax.fori_loop(1, 64, end, 0)


def finish_kernel(attn_ref, new_ref, attn_out, new_out, attn_buf, new_buf, in_sem, out_sem):
    pieces = [(attn_ref, attn_buf, attn_out)]
    for layer in range(2):
        for r in range(3):
            rows = slice(24 * r, 24 * r + 24)
            pieces.append((new_ref.at[layer, rows], new_buf.at[layer, rows], new_out.at[layer, rows]))
    takes = [pltpu.make_async_copy(src, buf, in_sem.at[i]) for i, (src, buf, dst) in enumerate(pieces)]
    puts = [pltpu.make_async_copy(buf, dst, out_sem.at[i]) for i, (src, buf, dst) in enumerate(pieces)]
    for take in takes:
        take.start()
    for take, put in zip(takes, puts):
        take.wait()
        put.start()
    for put in puts:
        put.wait()


def local(hidden, norm_gain, q_weight, latent_down_weight, kva_rope, latent_norm_scale,
          key_value_up_weight, earlier_token_cache, span_lens, prior_lens, old_cache, block_slot):
    whole = pl.BlockSpec(memory_space=pl.ANY)
    vmem = pl.BlockSpec(memory_space=pltpu.VMEM)
    smem = pl.BlockSpec(memory_space=pltpu.SMEM)
    dma = pltpu.SemaphoreType.DMA
    attn_out, moved = pl.pallas_call(
        layer_kernel,
        out_shape=(jax.ShapeDtypeStruct((512, 256), BF), jax.ShapeDtypeStruct((2, 72, 8192), BF)),
        in_specs=[vmem, smem, smem, vmem, vmem] + [whole] * 7,
        out_specs=(vmem, whole),
        scratch_shapes=[
            pltpu.VMEM((2, 576, 1024), BF),
            pltpu.VMEM((8, 2, 576, 128), BF),
            pltpu.VMEM((2, 576, 1024), BF),
            pltpu.VMEM((8, 2, 8, 72, 128), BF),
            pltpu.VMEM((8, 64, 2048), BF),
            pltpu.VMEM((8, 64, 2048), BF),
            pltpu.VMEM((2048, 384), BF),
            pltpu.VMEM((64, 2048), BF),
            pltpu.VMEM((512, 512), BF),
            pltpu.VMEM((576, 1024), BF),
            pltpu.VMEM((2, 256, 1536), BF),
            pltpu.VMEM((2, 128, 1536), BF),
            pltpu.VMEM((2, 512, 256), BF),
            pltpu.VMEM((8, 64, 2048), BF),
            pltpu.VMEM((4, 256, 1024), BF),
            pltpu.VMEM((4, 1024, 256), BF),
            dma((7,)), dma((2, 4, 2)), dma((2, 4, 2)), dma((2, 8)), dma((2, 8)), dma((2, 64)), dma((2, 64)),
            dma((3, 8)), dma((3, 8)), dma((4,)),
        ],
        compiler_params=pltpu.CompilerParams(collective_id=0, has_side_effects=True, vmem_limit_bytes=56 << 20),
    )(
        block_slot, span_lens, prior_lens, norm_gain, latent_norm_scale,
        hidden, jnp.swapaxes(old_cache, 1, 2), q_weight, latent_down_weight.T, kva_rope.T,
        key_value_up_weight, earlier_token_cache.T,
    )
    attn_out, moved = pl.pallas_call(
        finish_kernel,
        out_shape=(jax.ShapeDtypeStruct((512, 256), BF), jax.ShapeDtypeStruct((2, 72, 8192), BF)),
        in_specs=[whole, whole],
        out_specs=(whole, whole),
        scratch_shapes=[pltpu.VMEM((512, 256), BF), pltpu.VMEM((2, 72, 8192), BF), dma((7,)), dma((7,))],
    )(attn_out, moved)
    return attn_out, jnp.swapaxes(moved, 1, 2)


def solution(mesh):
    in_specs = (
        P(("group", "tensor"), None),
        P(),
        P(None, "tensor"),
        P(None, "tensor"),
        P(),
        P(),
        P(None, "tensor"),
        P("group", None),
        P("group", None),
        P("group", None),
        P(None, ("group", "tensor"), None),
        P(("group", "tensor"), None),
    )
    out_specs = (P("group", "tensor"), P(None, "group", "tensor"))
    return jax.shard_map(local, mesh=mesh, in_specs=in_specs, out_specs=out_specs, check_vma=False)
```

```python
import jax
import jax.numpy as jnp
from jax import lax
from jax.experimental import pallas as pl
from jax.experimental.pallas import tpu as pltpu
from jax.sharding import PartitionSpec as P

MESH = pl.DeviceIdType.MESH
BF = jnp.bfloat16
F32 = jnp.float32
EPS = 1e-06
LOG_BASE = 9.210340371976184
SCALE = 192 ** (-0.5)


def layer_kernel(slots_ref, span_ref, prior_ref, gain_ref, scale_ref,
                 hidden_ref, old_ref, qw_ref, latw_ref, kva_ref, up_ref, cache_ref,
                 attn_ref, new_ref,
                 own, arranged, landed, mid, hall, nrm, qw, kva, up, cache, keys, vals, qcat, wall, pick, swap,
                 load_sem, ag_send, ag_recv, a_send, a_recv, b_send, b_recv, w_send, w_recv, out_sem):
    g = lax.axis_index("group")
    t = lax.axis_index("tensor")
    z, xc = g // 8, g % 8
    x, c = xc // 2, xc % 2
    right, left = lax.rem(t + 1, 8), lax.rem(t + 7, 8)

    def side(k):
        return lax.rem(x + k // 2, 4) * 2 + lax.rem(c + k % 2, 2)

    piece = pl.ds(pl.multiple_of((z * 2 + c) * 128, 128), 128)
    loads = [pltpu.make_async_copy(src, dst, load_sem.at[i]) for i, (src, dst) in enumerate([
        (old_ref, own), (hidden_ref, hall.at[t]), (up_ref, up), (cache_ref, cache),
        (latw_ref.at[:, piece], wall.at[t, :, piece]), (kva_ref, kva), (qw_ref, qw)])]
    for load in loads:
        load.start()

    barrier = pltpu.get_barrier_semaphore()
    for k in range(1, 8):
        pl.semaphore_signal(barrier, inc=1, device_id=(z * 8 + side(k), t), device_id_type=MESH)

    def greet(k, carry):
        zz, tt = lax.rem(z + k // 8, 8), lax.rem(t + k % 8, 8)
        pl.semaphore_signal(barrier, inc=1, device_id=(zz * 8 + xc, tt), device_id_type=MESH)
        return carry

    lax.fori_loop(1, 64, greet, 0)
    pl.semaphore_wait(barrier, 70)

    def hop(way, step, half):
        owner = lax.rem(t + (8 - step if way == 0 else step), 8)
        rows = pl.ds(half * 32, 32)
        src = hidden_ref.at[rows] if step == 0 else hall.at[owner, rows]
        return pltpu.make_async_remote_copy(
            src_ref=src, dst_ref=hall.at[owner, rows],
            send_sem=ag_send.at[way, step, half], recv_sem=ag_recv.at[way, step, half],
            device_id=(g, right if way == 0 else left), device_id_type=MESH)

    hops = [[(w, s, h) for h in (0, 1) for w in (0, 1) if s < 3 or h == w] for s in range(4)]

    def pass_on(s):
        for w, _, h in hops[s]:
            hop(w, s, h).wait_recv()
            if s < 3 and (w, s + 1, h) in hops[s + 1]:
                hop(w, s + 1, h).start()

    for w, s, h in hops[0]:
        hop(w, s, h).start()

    def w_copy(stage, k):
        if stage == 0:
            peer, src, dst = (g, lax.rem(t + k, 8)), latw_ref.at[:, piece], wall.at[t, :, piece]
        elif stage == 1:
            peer, src, dst = (lax.rem(z + k, 8) * 8 + xc, t), wall.at[:, :, piece], wall.at[:, :, piece]
        else:
            cols = pl.ds(pl.multiple_of((lax.rem(z + 8 - k, 8) * 2 + c) * 128, 128), 128)
            peer, src, dst = (z * 8 + side(1), t), wall.at[:, :, cols], wall.at[:, :, cols]
        return pltpu.make_async_remote_copy(
            src_ref=src, dst_ref=dst, send_sem=w_send.at[stage, k], recv_sem=w_recv.at[stage, k],
            device_id=peer, device_id_type=MESH)

    for k in (4, 3, 5, 2, 6, 1, 7):
        w_copy(0, k).start()

    slots = jnp.broadcast_to(slots_ref[...], (8, 64))
    spread = (lax.broadcasted_iota(jnp.int32, (1024, 64), 0) // 16
              == lax.broadcasted_iota(jnp.int32, (1024, 64), 1)).astype(BF)
    slot_of = lax.dot_general(spread, slots.astype(F32).astype(BF), (((1,), (1,)), ((), ())),
                              preferred_element_type=F32)[:, 0:1].astype(jnp.int32)
    code_of = slot_of * 16 + lax.broadcasted_iota(jnp.int32, (1024, 1), 0) % 16
    code_of = jnp.broadcast_to(code_of, (1024, 256))
    lane = lax.broadcasted_iota(jnp.int32, (1, 256), 1)

    seat = pl.ds(pl.multiple_of(xc * 128, 128), 128)

    def a_copy(layer, k):
        return pltpu.make_async_remote_copy(
            src_ref=arranged.at[side(k), layer], dst_ref=landed.at[layer, :, seat],
            send_sem=a_send.at[layer, k], recv_sem=a_recv.at[layer, k],
            device_id=(z * 8 + side(k), t), device_id_type=MESH)

    loads[0].wait()
    stay = []
    for pair in range(4):
        want = ((lane % 128) // 16 * 8 + pair * 2 + lane // 128) * 16 + lane % 16
        pick[pair] = (code_of == jnp.broadcast_to(want, (1024, 256))).astype(BF)
    for layer in range(2):
        for pair in range(4):
            got = jnp.dot(own[layer], pick[pair], preferred_element_type=F32).astype(BF)
            arranged[2 * pair, layer] = got[:, :128]
            arranged[2 * pair + 1, layer] = got[:, 128:]
        for k in (4, 5, 2, 6, 3, 7, 1):
            a_copy(layer, k).start()
        stay.append(pltpu.make_async_copy(arranged.at[xc, layer], landed.at[layer, :, seat], out_sem.at[layer]))
        stay[layer].start()
        if layer == 0:
            pass_on(0)
            loads[4].wait()
            for k in range(1, 8):
                w_copy(0, k).wait_recv()
            for k in (4, 3, 5, 2, 6, 1, 7):
                w_copy(1, k).start()

    gain = gain_ref[...].reshape(1, 2048).astype(F32)

    def norm_rows(owner):
        rows = hall[owner].astype(F32)
        mean_sq = jnp.mean(rows * rows, axis=-1, keepdims=True)
        nrm[owner] = (rows * lax.rsqrt(mean_sq + EPS) * gain).astype(BF)

    row = lax.broadcasted_iota(jnp.int32, (1024, 256), 0)
    col = lax.broadcasted_iota(jnp.int32, (1, 256), 1)
    for pair in range(4):
        want = (col % 128) // 16 * 128 + (pair * 2 + col // 128) * 16 + col % 16
        swap[pair] = (row == jnp.broadcast_to(want, (1024, 256))).astype(BF)
    pass_on(1)
    loads[1].wait()
    norm_rows(t)
    norm_rows(left)
    norm_rows(right)
    norm_rows(lax.rem(t + 6, 8))
    norm_rows(lax.rem(t + 2, 8))
    pass_on(2)

    place = pl.ds(pl.multiple_of((t * 8 + z) * 128, 128), 128)

    def b_copy(layer, dz, dt):
        zz, tt = lax.rem(z + dz, 8), lax.rem(t + dt, 8)
        return pltpu.make_async_remote_copy(
            src_ref=mid.at[zz, layer, tt], dst_ref=new_ref.at[layer, :, place],
            send_sem=b_send.at[layer, dz * 8 + dt], recv_sem=b_recv.at[layer, dz * 8 + dt],
            device_id=(zz * 8 + xc, tt), device_id_type=MESH)

    keeps = []

    def send_layer(layer):
        stay[layer].wait()
        for k in range(1, 8):
            a_copy(layer, k).wait_recv()
        for pair in range(4):
            got = jnp.dot(landed[layer], swap[pair], preferred_element_type=F32).astype(BF)
            for u in range(8):
                mid[2 * pair, layer, u] = got[u * 72:(u + 1) * 72, :128]
                mid[2 * pair + 1, layer, u] = got[u * 72:(u + 1) * 72, 128:]

        def go(i, carry):
            far = (i >= 12).astype(jnp.int32)
            p = 1 + i // 4
            q = lax.rem(i, 4) + far
            for dz, dt in ((p, q), (8 - p, lax.rem(8 - q, 8)), (q, 8 - p), (lax.rem(8 - q, 8), p)):
                b_copy(layer, dz, dt).start()
            return carry

        lax.fori_loop(0, 15, go, 0)
        for dz, dt in ((4, 0), (0, 4), (4, 4)):
            b_copy(layer, dz, dt).start()
        keep = pltpu.make_async_copy(mid.at[z, layer, t], new_ref.at[layer, :, place], out_sem.at[2 + layer])
        keep.start()
        keeps.append(keep)

    send_layer(0)
    norm_rows(lax.rem(t + 5, 8))
    norm_rows(lax.rem(t + 3, 8))
    for load in loads[2:4]:
        load.wait()
    up_t = jnp.transpose(up[...].astype(F32)).astype(BF)

    def expand(latent_t, cols):
        wide = jnp.dot(up_t, latent_t, preferred_element_type=F32).astype(BF)
        for head in range(2):
            keys[head, 0:128, cols] = wide[head * 256:head * 256 + 128]
            vals[head, :, cols] = wide[head * 256 + 128:head * 256 + 256]

    for part in range(2):
        cols = slice(part * 512, part * 512 + 512)
        expand(cache[0:512, cols], cols)
        for head in range(2):
            keys[head, 128:192, cols] = cache[512:576, cols]
            keys[head, 192:256, cols] = cache[512:576, cols]

    spans = [span_ref[0, r] for r in range(8)]
    priors = [prior_ref[0, r] for r in range(8)]
    starts = [jnp.int32(0)]
    for r in range(7):
        starts.append(starts[r] + spans[r])

    def places(token):
        start, prior, request = jnp.zeros_like(token), jnp.zeros_like(token) + priors[0], jnp.zeros_like(token)
        for r in range(1, 8):
            inside = token >= starts[r]
            start = jnp.where(inside, starts[r], start)
            prior = jnp.where(inside, priors[r], prior)
            request = jnp.where(inside, r, request)
        return start, prior, request

    token = lax.broadcasted_iota(jnp.int32, (32, 512), 1)
    start, prior, _ = places(token)
    position = (prior + token - start).astype(F32)
    pair_of = lax.broadcasted_iota(jnp.int32, (32, 512), 0).astype(F32)
    angle = position * jnp.exp(pair_of * (-2.0 / 64 * LOG_BASE))
    cosine, sine = jnp.cos(angle), jnp.sin(angle)

    def rotate(rows):
        first, second = rows[0:32], rows[32:64]
        return [first * cosine - second * sine, second * cosine + first * sine]

    send_layer(1)

    pass_on(3)
    norm_rows(lax.rem(t + 4, 8))

    normed = nrm[...].reshape(512, 2048)
    w_copy(2, 0).start()
    for k in (1, 7, 2, 6, 3, 5, 4):
        w_copy(1, k).wait_recv()
        w_copy(2, k).start()

    loads[5].wait()
    rotary_new = lax.dot_general(kva[...], normed, (((1,), (1,)), ((), ())), preferred_element_type=F32)
    rotary_new = jnp.concatenate(rotate(rotary_new), axis=0).astype(BF)
    for head in range(2):
        keys[head, 128:192, 1024:1536] = rotary_new
        keys[head, 192:256, 1024:1536] = rotary_new

    loads[6].wait()
    query = jnp.dot(normed, qw[...], preferred_element_type=F32)
    turned = jnp.transpose(jnp.concatenate([query[:, 128:192], query[:, 320:384]], axis=1))
    turned = jnp.transpose(jnp.concatenate(rotate(turned[0:64]) + rotate(turned[64:128]), axis=0))
    half = lax.broadcasted_iota(jnp.int32, (512, 128), 1) // 64
    for head in range(2):
        qcat[head, :, 0:128] = query[:, head * 192:head * 192 + 128].astype(BF)
        qcat[head, :, 128:256] = jnp.where(half == head, turned, 0.0).astype(BF)

    for k in range(8):
        w_copy(2, k).wait_recv()
    latent = lax.dot_general(wall[...].reshape(512, 2048), normed, (((1,), (1,)), ((), ())),
                             preferred_element_type=F32)
    mean_sq = jnp.mean(latent * latent, axis=0, keepdims=True)
    scale = jnp.transpose(jnp.broadcast_to(scale_ref[...].reshape(1, 512).astype(F32), (128, 512)))
    scale = jnp.concatenate([scale] * 4, axis=1)
    expand((latent * lax.rsqrt(mean_sq + EPS) * scale).astype(BF), slice(1024, 1536))

    def attend(block, carry):
        rows = pl.ds(pl.multiple_of(block * 128, 128), 128)
        mine = lax.broadcasted_iota(jnp.int32, (128, 1), 0) + block * 128
        start, prior, request = places(mine)
        key = lax.broadcasted_iota(jnp.int32, (128, 1536), 1)
        allowed = ((key >= request * 128) & (key < request * 128 + prior)) | (
            (key >= start + 1024) & (key <= mine + 1024))
        for head in range(2):
            scores = jnp.dot(qcat[head, rows, :], keys[head], preferred_element_type=F32) * SCALE
            scores = jnp.where(allowed, scores, -jnp.inf)
            weights = jnp.exp(scores - jnp.max(scores, axis=-1, keepdims=True))
            probs = (weights / jnp.sum(weights, axis=-1, keepdims=True)).astype(BF)
            mixed = lax.dot_general(probs, vals[head], (((1,), (1,)), ((), ())), preferred_element_type=F32)
            attn_ref[rows, head * 128:head * 128 + 128] = mixed.astype(BF)
        return carry

    lax.fori_loop(0, 4, attend, 0)

    for s in range(4):
        for w, _, h in hops[s]:
            hop(w, s, h).wait_send()
    for stage in range(3):
        for k in range(1 if stage < 2 else 0, 8):
            w_copy(stage, k).wait_send()
    for layer in range(2):
        keeps[layer].wait()
        for k in range(1, 8):
            a_copy(layer, k).wait_send()

        def end(k, carry):
            copy = b_copy(layer, k // 8, lax.rem(k, 8))
            copy.wait_send()
            copy.wait_recv()
            return carry

        lax.fori_loop(1, 64, end, 0)


def finish_kernel(attn_ref, new_ref, attn_out, new_out, attn_buf, new_buf, in_sem, out_sem):
    pieces = [(attn_ref, attn_buf, attn_out)]
    for layer in range(2):
        for r in range(3):
            rows = slice(24 * r, 24 * r + 24)
            pieces.append((new_ref.at[layer, rows], new_buf.at[layer, rows], new_out.at[layer, rows]))
    takes = [pltpu.make_async_copy(src, buf, in_sem.at[i]) for i, (src, buf, dst) in enumerate(pieces)]
    puts = [pltpu.make_async_copy(buf, dst, out_sem.at[i]) for i, (src, buf, dst) in enumerate(pieces)]
    for take in takes:
        take.start()
    for take, put in zip(takes, puts):
        take.wait()
        put.start()
    for put in puts:
        put.wait()


def local(hidden, norm_gain, q_weight, latent_down_weight, kva_rope, latent_norm_scale,
          key_value_up_weight, earlier_token_cache, span_lens, prior_lens, old_cache, block_slot):
    whole = pl.BlockSpec(memory_space=pl.ANY)
    vmem = pl.BlockSpec(memory_space=pltpu.VMEM)
    smem = pl.BlockSpec(memory_space=pltpu.SMEM)
    dma = pltpu.SemaphoreType.DMA
    attn_out, moved = pl.pallas_call(
        layer_kernel,
        out_shape=(jax.ShapeDtypeStruct((512, 256), BF), jax.ShapeDtypeStruct((2, 72, 8192), BF)),
        in_specs=[vmem, smem, smem, vmem, vmem] + [whole] * 7,
        out_specs=(vmem, whole),
        scratch_shapes=[
            pltpu.VMEM((2, 576, 1024), BF),
            pltpu.VMEM((8, 2, 576, 128), BF),
            pltpu.VMEM((2, 576, 1024), BF),
            pltpu.VMEM((8, 2, 8, 72, 128), BF),
            pltpu.VMEM((8, 64, 2048), BF),
            pltpu.VMEM((8, 64, 2048), BF),
            pltpu.VMEM((2048, 384), BF),
            pltpu.VMEM((64, 2048), BF),
            pltpu.VMEM((512, 512), BF),
            pltpu.VMEM((576, 1024), BF),
            pltpu.VMEM((2, 256, 1536), BF),
            pltpu.VMEM((2, 128, 1536), BF),
            pltpu.VMEM((2, 512, 256), BF),
            pltpu.VMEM((8, 64, 2048), BF),
            pltpu.VMEM((4, 1024, 256), BF),
            pltpu.VMEM((4, 1024, 256), BF),
            dma((7,)), dma((2, 4, 2)), dma((2, 4, 2)), dma((2, 8)), dma((2, 8)), dma((2, 64)), dma((2, 64)),
            dma((3, 8)), dma((3, 8)), dma((4,)),
        ],
        compiler_params=pltpu.CompilerParams(collective_id=0, has_side_effects=True, vmem_limit_bytes=56 << 20),
    )(
        block_slot, span_lens, prior_lens, norm_gain, latent_norm_scale,
        hidden, jnp.swapaxes(old_cache, 1, 2), q_weight, latent_down_weight.T, kva_rope.T,
        key_value_up_weight, earlier_token_cache.T,
    )
    attn_out, moved = pl.pallas_call(
        finish_kernel,
        out_shape=(jax.ShapeDtypeStruct((512, 256), BF), jax.ShapeDtypeStruct((2, 72, 8192), BF)),
        in_specs=[whole, whole],
        out_specs=(whole, whole),
        scratch_shapes=[pltpu.VMEM((512, 256), BF), pltpu.VMEM((2, 72, 8192), BF), dma((7,)), dma((7,))],
    )(attn_out, moved)
    return attn_out, jnp.swapaxes(moved, 1, 2)


def solution(mesh):
    in_specs = (
        P(("group", "tensor"), None),
        P(),
        P(None, "tensor"),
        P(None, "tensor"),
        P(),
        P(),
        P(None, "tensor"),
        P("group", None),
        P("group", None),
        P("group", None),
        P(None, ("group", "tensor"), None),
        P(("group", "tensor"), None),
    )
    out_specs = (P("group", "tensor"), P(None, "group", "tensor"))
    return jax.shard_map(local, mesh=mesh, in_specs=in_specs, out_specs=out_specs, check_vma=False)
```
